32 devices in a mesh: dp: 8 (over z, y), mp: 4 (over x, core).
Axes of the slice: x: 2, y: 2, z: 4, core: 2. Of those that a mesh axis runs over, the one named last changes fastest.
Arguments:
- tokens: bfloat16 [8192, 768], P(('dp', 'mp')), may hold values from -6 to 6
- segment_ids: int32 [8192], P('dp'), may hold values from 0 to 10, as said below
- keep_mask: int32 [88, 2], P('dp'), may hold values 0 or 1
- first_gain: bfloat16 [768], replicated, may hold values from 0.5 to 1.5
- first_shift: bfloat16 [768], replicated, may hold values from -3 to 3
- query_weight: bfloat16 [768, 768], P(None, 'mp'), may hold values from -0.21875 to 0.21875
- query_bias: bfloat16 [768], P('mp'), may hold values from -3 to 3
- key_weight: bfloat16 [768, 768], P(None, 'mp'), may hold values from -0.21875 to 0.21875
- value_weight: bfloat16 [768, 768], P(None, 'mp'), may hold values from -0.21875 to 0.21875
- value_bias: bfloat16 [768], P('mp'), may hold values from -3 to 3
- out_weight: bfloat16 [768, 768], P('mp'), may hold values from -2.5 to 2.5
- out_bias: bfloat16 [768], replicated, may hold values from -2 to 2
- second_gain: bfloat16 [768], replicated, may hold values from 0.5 to 1.5
- second_shift: bfloat16 [768], replicated, may hold values from -3 to 3
- up_weight: bfloat16 [768, 3072], P(None, 'mp'), may hold values from -0.21875 to 0.21875
- up_bias: bfloat16 [3072], P('mp'), may hold values from -3 to 3
- down_weight: bfloat16 [3072, 768], P('mp'), may hold values from -0.109375 to 0.109375
- down_bias: bfloat16 [768], replicated, may hold values from -2 to 2
- cotangent: bfloat16 [8192, 768], P(('dp', 'mp')), may hold values from -6 to 6
Outputs:
- layer_out: bfloat16 [8192, 768], P(('dp', 'mp'))
- input_grad: float32 [8192, 768], P(('dp', 'mp'))
- first_gain_grad: float32 [768], replicated
- first_shift_grad: float32 [768], replicated
- query_weight_grad: float32 [768, 768], P(None, 'mp')
- query_bias_grad: float32 [768], P('mp')
- key_weight_grad: float32 [768, 768], P(None, 'mp')
- value_weight_grad: float32 [768, 768], P(None, 'mp')
- value_bias_grad: float32 [768], P('mp')
- out_weight_grad: float32 [768, 768], P('mp')
- out_bias_grad: float32 [768], replicated
- second_gain_grad: float32 [768], replicated
- second_shift_grad: float32 [768], replicated
- up_weight_grad: float32 [768, 3072], P(None, 'mp')
- up_bias_grad: float32 [3072], P('mp')
- down_weight_grad: float32 [3072, 768], P('mp')
- down_bias_grad: float32 [768], replicated
The draws below stay inside these ranges and needn't reach their ends.
Inputs may be any that keep to these rules, and one draw needn't show every extreme that they name: `segment_ids`: within each aligned block of 1024 tokens the ids start at 0, never fall and rise by one from image to image; every image but the last of a block has 102, 198 or 578 tokens, the last holds the remaining tokens. In the first block every image but the last has 102 tokens. `keep_mask`: row i of a block of 11 rows belongs to the image with segment id i of the same index of dp.
All inputs are finite; a program needn't handle non-finite values.
Results may differ from the reference program's by a relative error of at most 0.02.
Values may be sent and summed in bfloat16 or wider, within the bound.
No kernel may reach another device: no remote copies, remote signals or barrier semaphores. Data moves between devices by JAX's collectives and lax.ppermute only.
A program may use at most 128 MiB of HBM per device.

```python
import math
import jax
import jax.numpy as jnp
from jax import lax

D = 768
HEADS = 12
HD = 64
FF = 3072
TOK_DP = 1024
SHORT = 102
MID = 198
LONG = 578
IMGS = 11
TOKENS = 8192
IMAGES = 88
N_DP = 8
N_MP = 4


def draw_segment_ids(key, part):
    groups = TOKENS // TOK_DP
    image_kind = jax.random.randint(key, (groups, IMGS), 0, 3)
    first_block = (jnp.arange(groups, dtype=jnp.int32) == 0)[:, None]
    image_kind = jnp.where(first_block, 0, image_kind).astype(jnp.int32)
    lengths = jnp.where(image_kind == 0, SHORT, jnp.where(image_kind == 1, MID, LONG)).astype(jnp.int32)
    bounds = jnp.cumsum(lengths, axis=1).astype(jnp.int32)
    positions = jnp.arange(TOK_DP, dtype=jnp.int32)
    image_ids = jnp.sum((bounds[:, None, :] <= positions[None, :, None]).astype(jnp.int32), axis=2)
    return image_ids.reshape(groups * TOK_DP).astype(jnp.int32)


def touch_ends(values, rng, least, high):
    longest = values.shape.index(max(values.shape))
    spots = []
    for shift in (0, 1):
        where = [jax.random.randint(jax.random.fold_in(rng, axis), (), 0, length) for axis, length in enumerate(values.shape)]
        where[longest] = (where[longest] + shift) % values.shape[longest]
        spots.append(tuple(where))
    return values.at[spots[0]].set(least).at[spots[1]].set(high)


def level_of(stream_key, dims, pieces, least, top_value):
    loudness, own = 1.0, jax.random.fold_in(stream_key, 6)
    for dim, shards_of in pieces:
        heights = jnp.exp(jax.random.uniform(jax.random.fold_in(own, dim), (shards_of,), jnp.float32, least / len(pieces), top_value / len(pieces)))
        loudness = loudness * jnp.repeat(heights, dims[dim] // shards_of).reshape([-1 if axis == dim else 1 for axis in range(len(dims))])
    return loudness


def centred(key, shape, scale, limit, shards=(), kind=jnp.bfloat16):
    entries = jax.random.normal(key, shape, jnp.float32) * scale
    if len(shards) > 0:
        entries = level_of(key, shape, shards, -0.22, 0.18) * entries
    return jnp.clip(entries, min=-limit, max=limit).astype(kind)


def setup_inputs(seed: int = 0) -> dict:
    key_of = jax.random.split(jax.random.key(seed), 20)
    tokens = centred(key_of[0], (TOKENS, D), 1.0, 6.0, ((0, 32),))
    segment_ids = draw_segment_ids(jax.random.fold_in(key_of[19], 71), 0)
    keep_mask = touch_ends((jax.random.randint(key_of[2], (IMAGES, 2), 0, 10) < 9).astype(jnp.int32), jax.random.fold_in(key_of[2], 1), 0, 1)
    first_gain = jnp.clip(1.0 + 0.1 * jax.random.normal(key_of[3], (D,), jnp.float32), 0.5, 1.5).astype(jnp.bfloat16)
    first_shift = centred(key_of[4], (D,), 0.5, 3.0)
    query_weight = centred(key_of[5], (D, D), D ** -0.5, 0.21875, ((1, 4),))
    query_bias = centred(key_of[6], (D,), 0.5, 3.0, ((0, 4),))
    key_weight = centred(key_of[7], (D, D), D ** -0.5, 0.21875, ((1, 4),))
    value_weight = centred(key_of[8], (D, D), D ** -0.5, 0.21875, ((1, 4),))
    value_bias = centred(key_of[9], (D,), 0.5, 3.0, ((0, 4),))
    out_weight = centred(key_of[10], (D, D), (max(D // 128, 1)) ** -0.5, 2.5, ((0, 4),))
    out_bias = centred(key_of[11], (D,), 0.3, 2.0)
    second_gain = jnp.clip(1.0 + 0.1 * jax.random.normal(key_of[12], (D,), jnp.float32), 0.5, 1.5).astype(jnp.bfloat16)
    second_shift = centred(key_of[13], (D,), 0.5, 3.0)
    up_weight = centred(key_of[14], (D, FF), D ** -0.5, 0.21875, ((1, 4),))
    up_bias = centred(key_of[15], (FF,), 0.5, 3.0, ((0, 4),))
    down_weight = centred(key_of[16], (FF, D), FF ** -0.5, 0.109375, ((0, 4),))
    down_bias = centred(key_of[17], (D,), 0.3, 2.0)
    cotangent = centred(key_of[18], (TOKENS, D), 1.0, 6.0, ((0, 32),))
    return dict(tokens=tokens, segment_ids=segment_ids, keep_mask=keep_mask, first_gain=first_gain, first_shift=first_shift, query_weight=query_weight, query_bias=query_bias, key_weight=key_weight, value_weight=value_weight, value_bias=value_bias, out_weight=out_weight, out_bias=out_bias, second_gain=second_gain, second_shift=second_shift, up_weight=up_weight, up_bias=up_bias, down_weight=down_weight, down_bias=down_bias, cotangent=cotangent)


eps = 1e-06

@jax.custom_vjp
def low(v):
    return lax.optimization_barrier(v.astype(jnp.bfloat16)).astype(jnp.float32)

@jax.custom_vjp
def low_back(v):
    return v

def low_keep(v):
    return (low(v), None)

def low_pass(kept, grad):
    return (grad,)

def back_keep(v):
    return (v, None)

def back_low(kept, grad):
    return (low(grad),)
low.defvjp(low_keep, low_pass)
low_back.defvjp(back_keep, back_low)

def both_round(values):
    return low(low_back(values))

def product(left, right):
    return jnp.dot(left, right, precision=lax.Precision.HIGHEST, preferred_element_type=jnp.float32)

def layer_norm(values, scaling, bias_add):
    center = values - lax.optimization_barrier(jnp.mean(values, axis=-1, keepdims=True))
    spread = lax.optimization_barrier(jnp.mean(center * center, axis=-1, keepdims=True))
    return center * lax.rsqrt(spread + eps) * scaling + bias_add

def group_layer(weight_list, group_rows, group_ids, group_slots):
    first_gain, first_shift, query_weight, query_bias, key_weight, value_weight, value_bias, out_weight, out_bias, second_gain, second_shift, up_weight, up_bias, down_weight, down_bias = weight_list
    row_count = group_rows.shape[0]
    head_width = D // N_MP
    hidden_width = FF // N_MP
    head_group = HEADS // N_MP
    score_scale = 1.0 / math.sqrt(HD)
    onehot = (group_ids[:, None] == jnp.arange(group_slots.shape[0], dtype=jnp.int32)[None, :]).astype(jnp.float32)
    keep_rows = product(onehot, group_slots) / 0.9
    allowed = group_ids[:, None] == group_ids[None, :]
    normed = low(layer_norm(group_rows, first_gain, first_shift))
    out_terms = []
    for member in range(N_MP):
        inputs = low_back(normed)
        column_range = slice(member * head_width, (member + 1) * head_width)
        query_rows = both_round(product(inputs, query_weight[:, column_range]) + query_bias[column_range])
        key_rows = both_round(product(inputs, key_weight[:, column_range]))
        value_rows = both_round(product(inputs, value_weight[:, column_range]) + value_bias[column_range])
        query_rows = query_rows.reshape(row_count, head_group, HD)
        key_rows = key_rows.reshape(row_count, head_group, HD)
        value_rows = value_rows.reshape(row_count, head_group, HD)
        scores = low_back(jnp.einsum('qhd,khd->hqk', query_rows, key_rows, precision=lax.Precision.HIGHEST) * score_scale)
        scores = jnp.where(allowed[None], scores, -1e+30)
        weights = jax.nn.softmax(scores, axis=-1)
        context = jnp.einsum('hqk,khd->qhd', low(weights), value_rows, precision=lax.Precision.HIGHEST)
        context = both_round(context.reshape(row_count, head_width))
        out_terms.append(low(product(context, out_weight[column_range, :])))
    attended = low_back(sum(out_terms)) + out_bias
    middle = group_rows + keep_rows[:, 0:1] * attended
    normed_two = low(layer_norm(middle, second_gain, second_shift))
    mlp_terms = []
    for member in range(N_MP):
        inputs = low_back(normed_two)
        hidden_range = slice(member * hidden_width, (member + 1) * hidden_width)
        hidden = low_back(product(inputs, up_weight[:, hidden_range]) + up_bias[hidden_range])
        activated = low(jax.nn.gelu(hidden, approximate=False))
        mlp_terms.append(low(product(activated, down_weight[hidden_range, :])))
    mlp_out = low_back(sum(mlp_terms)) + down_bias
    return middle + keep_rows[:, 1:2] * mlp_out

def forward_all(all_rows, weight_list, segment_ids, keep_slots):
    stacked = (all_rows.reshape(N_DP, TOK_DP, D), segment_ids.reshape(N_DP, TOK_DP), keep_slots.reshape(N_DP, IMGS, 2))
    group_fn = jax.checkpoint(lambda group_rows, group_ids, group_slots: group_layer(weight_list, group_rows, group_ids, group_slots))

    def scan_step(unused_carry, group_item):
        return (unused_carry, group_fn(group_item[0], group_item[1], group_item[2]))
    unused_carry, group_outs = lax.scan(scan_step, jnp.zeros((), jnp.float32), stacked)
    return group_outs.reshape(TOKENS, D)

def reference(tokens, segment_ids, keep_mask, first_gain, first_shift, query_weight, query_bias, key_weight, value_weight, value_bias, out_weight, out_bias, second_gain, second_shift, up_weight, up_bias, down_weight, down_bias, cotangent):
    weight_list = tuple((item.astype(jnp.float32) for item in (first_gain, first_shift, query_weight, query_bias, key_weight, value_weight, value_bias, out_weight, out_bias, second_gain, second_shift, up_weight, up_bias, down_weight, down_bias)))
    keep_slots = keep_mask.astype(jnp.float32)

    def wrapped(all_rows, *weights):
        return forward_all(all_rows, weights, segment_ids, keep_slots)
    layer_out, pullback = jax.vjp(wrapped, tokens.astype(jnp.float32), *weight_list)
    gradients = pullback(cotangent.astype(jnp.float32))
    return (layer_out.astype(jnp.bfloat16), gradients[0], gradients[1], gradients[2], gradients[3], gradients[4], gradients[5], gradients[6], gradients[7], gradients[8], gradients[9], gradients[10], gradients[11], gradients[12], gradients[13], gradients[14], gradients[15])
```

```python
import math

import jax
import jax.numpy as jnp
from jax import lax
from jax.sharding import PartitionSpec as P

HD = 64
eps = 1e-06
f32 = jnp.float32
bf16 = jnp.bfloat16


def bits_of(size):
    return [1 << b for b in range(size.bit_length() - 1)]


def swap(values, axis, bit, size):
    return lax.ppermute(values, axis, [(i, i ^ bit) for i in range(size)])


def rel_order(size):
    order = [0]
    for bit in reversed(bits_of(size)):
        order = order + [o ^ bit for o in order]
    return order


def gather_mp(block, size):
    blocks = [block]
    for bit in reversed(bits_of(size)):
        blocks = blocks + [swap(b, "mp", bit, size) for b in blocks]
    return blocks


def scatter_mp(part, size):
    total = part
    for bit in bits_of(size):
        half = total.shape[0] // 2
        got = swap(total[half:].astype(bf16), "mp", bit, size)
        total = total[:half].astype(f32) + got.astype(f32)
    return total


def reduce_dp(values, size):
    index = lax.axis_index("dp")
    total = values
    for bit in bits_of(size):
        half = total.shape[0] // 2
        side = (index // bit) % 2
        keep = lax.dynamic_slice_in_dim(total, side * half, half)
        send = lax.dynamic_slice_in_dim(total, (1 - side) * half, half).astype(bf16)
        total = keep.astype(f32) + swap(send, "dp", bit, size).astype(f32)
    total = total.astype(bf16)
    for bit in reversed(bits_of(size)):
        half = total.shape[0]
        side = (index // bit) % 2
        other = swap(total, "dp", bit, size)
        low = jnp.where(side == 0, total, other)
        high = jnp.where(side == 0, other, total)
        total = jnp.concatenate([low, high], axis=0)
    return total.astype(f32)


def layer_norm(values, scaling, bias_add):
    center = values - jnp.mean(values, axis=-1, keepdims=True)
    spread = jnp.mean(center * center, axis=-1, keepdims=True)
    return center * lax.rsqrt(spread + eps) * scaling + bias_add


def gelu_exact(values):
    return jax.nn.gelu(values, approximate=False)


def keep_of(ids, keep_mask):
    slots = jnp.arange(keep_mask.shape[0], dtype=jnp.int32)
    onehot = ids[:, None] == slots[None, :]
    flags = keep_mask.astype(f32)
    one = jnp.sum(jnp.where(onehot, flags[None, :, 0], 0.0), axis=1, keepdims=True)
    two = jnp.sum(jnp.where(onehot, flags[None, :, 1], 0.0), axis=1, keepdims=True)
    return one / 0.9, two / 0.9


def per_device(
    sizes,
    tokens,
    segment_ids,
    keep_mask,
    first_gain,
    first_shift,
    query_weight,
    query_bias,
    key_weight,
    value_weight,
    value_bias,
    out_weight,
    out_bias,
    second_gain,
    second_shift,
    up_weight,
    up_bias,
    down_weight,
    down_bias,
    cotangent,
):
    n_dp, n_mp = sizes
    local_rows = tokens.shape[0]
    row_count = segment_ids.shape[0]
    head_width = query_weight.shape[1]
    head_group = head_width // HD
    score_scale = 1.0 / math.sqrt(HD)
    block_rows = min(512, row_count)
    block_count = row_count // block_rows
    me = lax.axis_index("mp")
    token_all = jnp.concatenate(gather_mp(tokens, n_mp), axis=0)
    cot_all = jnp.concatenate(gather_mp(cotangent, n_mp), axis=0)
    ids_all = jnp.concatenate(
        [
            lax.dynamic_slice_in_dim(segment_ids, (me ^ r) * local_rows, local_rows)
            for r in rel_order(n_mp)
        ]
    )
    keep_one_all, keep_two_all = keep_of(ids_all, keep_mask)
    keep_one = keep_one_all[:local_rows]
    keep_two = keep_two_all[:local_rows]
    allowed = ids_all[:, None] == ids_all[None, :]
    gain_one = first_gain.astype(f32)
    shift_one = first_shift.astype(f32)
    gain_two = second_gain.astype(f32)
    shift_two = second_shift.astype(f32)
    inputs = tokens.astype(f32)
    normed_all = layer_norm(token_all.astype(f32), gain_one, shift_one).astype(bf16)
    query_rows = (
        jnp.dot(normed_all, query_weight, preferred_element_type=f32) + query_bias.astype(f32)
    ).astype(bf16)
    key_rows = jnp.dot(normed_all, key_weight, preferred_element_type=f32).astype(bf16)
    value_rows = (
        jnp.dot(normed_all, value_weight, preferred_element_type=f32) + value_bias.astype(f32)
    ).astype(bf16)
    key_heads = key_rows.reshape(row_count, head_group, HD)
    value_heads = value_rows.reshape(row_count, head_group, HD)
    context_parts = []
    lse_parts = []
    for number in range(block_count):
        row_start = number * block_rows
        query_block = query_rows[row_start : row_start + block_rows].reshape(
            block_rows, head_group, HD
        )
        scores = (
            jnp.einsum("qhd,khd->hqk", query_block, key_heads, preferred_element_type=f32)
            * score_scale
        )
        scores = jnp.where(allowed[row_start : row_start + block_rows][None], scores, -1e30)
        largest = jnp.max(scores, axis=-1, keepdims=True)
        powers = jnp.exp(scores - largest)
        totals = jnp.sum(powers, axis=-1, keepdims=True)
        weights = (powers / totals).astype(bf16)
        context_block = jnp.einsum("hqk,khd->qhd", weights, value_heads, preferred_element_type=f32)
        context_parts.append(context_block.reshape(block_rows, head_width))
        lse_parts.append(largest + jnp.log(totals))
    context = jnp.concatenate(context_parts, axis=0).astype(bf16)
    attended = scatter_mp(
        jnp.dot(context, out_weight, preferred_element_type=f32).astype(bf16), n_mp
    ) + out_bias.astype(f32)
    middle = inputs + keep_one * attended
    normed_two = layer_norm(middle, gain_two, shift_two).astype(bf16)
    normed_two_all = jnp.concatenate(gather_mp(normed_two, n_mp), axis=0)
    hidden = jnp.dot(normed_two_all, up_weight, preferred_element_type=f32) + up_bias.astype(f32)
    activated = gelu_exact(hidden).astype(bf16)
    mlp_out = scatter_mp(
        jnp.dot(activated, down_weight, preferred_element_type=f32).astype(bf16), n_mp
    ) + down_bias.astype(f32)
    layer_out = (middle + keep_two * mlp_out).astype(bf16)
    out_grad = cotangent.astype(f32)
    down_bias_grad = jnp.sum(out_grad * keep_two, axis=0)
    mlp_grad_all = (cot_all.astype(f32) * keep_two_all).astype(bf16)
    down_weight_grad = jnp.einsum("rf,rd->fd", activated, mlp_grad_all, preferred_element_type=f32)
    act_grad = jnp.einsum("rd,fd->rf", mlp_grad_all, down_weight, preferred_element_type=f32)
    unused_value, gelu_pull = jax.vjp(gelu_exact, hidden)
    hidden_grad = gelu_pull(act_grad)[0].astype(bf16)
    up_bias_grad = jnp.sum(hidden_grad.astype(f32), axis=0)
    up_weight_grad = jnp.einsum(
        "rd,rf->df", normed_two_all, hidden_grad, preferred_element_type=f32
    )
    second_grad = scatter_mp(
        jnp.einsum("rf,df->rd", hidden_grad, up_weight, preferred_element_type=f32).astype(bf16),
        n_mp,
    )
    down_weight_grad = reduce_dp(down_weight_grad, n_dp)
    up_weight_grad = reduce_dp(up_weight_grad, n_dp)
    unused_value, norm_pull_two = jax.vjp(layer_norm, middle, gain_two, shift_two)
    middle_part, gain_two_grad, shift_two_grad = norm_pull_two(second_grad)
    middle_grad = out_grad + middle_part
    attn_grad = middle_grad * keep_one
    out_bias_grad = jnp.sum(attn_grad, axis=0)
    attn_grad_all = jnp.concatenate(gather_mp(attn_grad.astype(bf16), n_mp), axis=0)
    out_weight_grad = jnp.einsum("rc,rd->cd", context, attn_grad_all, preferred_element_type=f32)
    out_weight_grad = reduce_dp(out_weight_grad, n_dp)
    context_grad = jnp.einsum(
        "rd,cd->rc", attn_grad_all, out_weight, preferred_element_type=f32
    ).astype(bf16)
    context_grad_heads = context_grad.reshape(row_count, head_group, HD)
    query_grads = []
    key_grad = jnp.zeros((row_count, head_group, HD), f32)
    value_grad = jnp.zeros((row_count, head_group, HD), f32)
    for number in range(block_count):
        row_start = number * block_rows
        query_block = query_rows[row_start : row_start + block_rows].reshape(
            block_rows, head_group, HD
        )
        scores = (
            jnp.einsum("qhd,khd->hqk", query_block, key_heads, preferred_element_type=f32)
            * score_scale
        )
        scores = jnp.where(allowed[row_start : row_start + block_rows][None], scores, -1e30)
        probs = jnp.exp(scores - lse_parts[number])
        grad_block = context_grad_heads[row_start : row_start + block_rows]
        prob_grad = jnp.einsum("qhd,khd->hqk", grad_block, value_heads, preferred_element_type=f32)
        center = jnp.sum(probs * prob_grad, axis=-1, keepdims=True)
        score_grad = (probs * (prob_grad - center)).astype(bf16)
        query_grads.append(
            jnp.einsum("hqk,khd->qhd", score_grad, key_heads, preferred_element_type=f32)
            * score_scale
        )
        key_grad = (
            key_grad
            + jnp.einsum("hqk,qhd->khd", score_grad, query_block, preferred_element_type=f32)
            * score_scale
        )
        value_grad = value_grad + jnp.einsum(
            "hqk,qhd->khd", probs.astype(bf16), grad_block, preferred_element_type=f32
        )
    query_grad_rows = (
        jnp.concatenate(query_grads, axis=0).reshape(row_count, head_width).astype(bf16)
    )
    key_grad_rows = key_grad.reshape(row_count, head_width).astype(bf16)
    value_grad_rows = value_grad.reshape(row_count, head_width).astype(bf16)
    query_bias_grad = jnp.sum(query_grad_rows.astype(f32), axis=0)
    value_bias_grad = jnp.sum(value_grad_rows.astype(f32), axis=0)
    qkv_grad = jnp.concatenate([query_grad_rows, key_grad_rows, value_grad_rows], axis=1)
    qkv_weight = jnp.concatenate([query_weight, key_weight, value_weight], axis=1)
    qkv_weight_grad = jnp.einsum("rd,rc->dc", normed_all, qkv_grad, preferred_element_type=f32)
    first_grad = scatter_mp(
        jnp.einsum("rc,dc->rd", qkv_grad, qkv_weight, preferred_element_type=f32).astype(bf16),
        n_mp,
    )
    qkv_weight_grad = reduce_dp(qkv_weight_grad, n_dp)
    unused_value, norm_pull_one = jax.vjp(layer_norm, inputs, gain_one, shift_one)
    input_part, gain_one_grad, shift_one_grad = norm_pull_one(first_grad)
    input_grad = middle_grad + input_part
    width = tokens.shape[1]
    small = jnp.stack(
        [gain_one_grad, shift_one_grad, out_bias_grad, gain_two_grad, shift_two_grad, down_bias_grad]
    )
    owned = jnp.concatenate([query_bias_grad, value_bias_grad, up_bias_grad])
    owned_size = owned.shape[0]
    owned_rows = -(-owned_size // width)
    owned = jnp.pad(owned, (0, owned_rows * width - owned_size)).reshape(owned_rows, width)
    sums = jnp.concatenate([small, owned], axis=0)
    for bit in bits_of(n_dp):
        sums = sums + swap(sums, "dp", bit, n_dp)
    small, owned = sums[:6], sums[6:].reshape(-1)
    for bit in bits_of(n_mp):
        small = small + swap(small, "mp", bit, n_mp)
    return (
        layer_out,
        input_grad,
        small[0],
        small[1],
        qkv_weight_grad[:, :head_width],
        owned[:head_width],
        qkv_weight_grad[:, head_width : 2 * head_width],
        qkv_weight_grad[:, 2 * head_width :],
        owned[head_width : 2 * head_width],
        out_weight_grad,
        small[2],
        small[3],
        small[4],
        up_weight_grad,
        owned[2 * head_width : owned_size],
        down_weight_grad,
        small[5],
    )


def solution(mesh):
    sizes = (mesh.shape["dp"], mesh.shape["mp"])

    def body(*args):
        return per_device(sizes, *args)

    rows = P(("dp", "mp"), None)
    cols = P(None, "mp")
    part = P("mp")
    in_specs = (
        rows, P("dp"), P("dp", None), P(), P(), cols, part, cols, cols, part, P("mp", None),
        P(), P(), P(), cols, part, P("mp", None), P(), rows,
    )
    out_specs = (
        rows, rows, P(), P(), cols, part, cols, cols, part, P("mp", None), P(), P(), P(),
        cols, part, P("mp", None), P(),
    )
    return jax.shard_map(body, mesh=mesh, in_specs=in_specs, out_specs=out_specs, check_vma=False)
```
